32 devices in a mesh: dp: 4 (over y, x), token: 8 (over z, core).
Axes of the slice: x: 2, y: 2, z: 4, core: 2. Of those that a mesh axis runs over, the one named last changes fastest.
Arguments:
- mix_input: bfloat16 [1536, 8, 768], P('dp', 'token'), may hold values from -6 to 6
- out_grad: bfloat16 [1536, 8, 768], P('dp', 'token'), may hold values from -1.5 to 1.5
- w_up: bfloat16 [8, 768, 3072], P('token'), may hold values from -0.21875 to 0.21875
- w_down: bfloat16 [8, 3072, 768], P('token'), may hold values from -0.109375 to 0.109375
- gain_first: float32 [8, 768], P('token'), may hold values from 0.25 to 1.75
- gain_second: float32 [8, 768], P('token'), may hold values from 0.25 to 1.75
- owner_dev: int32 [8, 1536, 1], P('token', 'dp'), may hold values from 0 to 3; in each aligned block of 384 rows (0 to 383, 384 to 767, ..., all dimensions but the last counted through in order) at most 240 rows name the same one
- slot_row: int32 [8, 1536], P('token', 'dp'), may hold values from 0 to 255
Outputs:
- grad_up: float32 [8, 768, 3072], P('token', 'dp')
- grad_down: float32 [8, 3072, 768], P('token', 'dp')
- row_grad: float32 [8, 1024, 768], P('token', 'dp')
The draws below stay inside these ranges and needn't reach their ends.
Inputs may be any that keep to these rules, and one draw needn't show every extreme that they name: `owner_dev`: in the rows of one device (aligned blocks of 384 samples of one token) no owner is named by more than 240 rows, a bound that some block reaches.
All inputs are finite; a program needn't handle non-finite values.
Results may differ from the reference program's by a relative error of at most 0.015.
Values may be sent and summed in bfloat16 or wider, within the bound.
A program may use at most 128 MiB of HBM per device.

```python
import math
import jax
import jax.numpy as jnp
import numpy as np
from jax import lax

D = 768
F = 3072
B_DEV = 384
HOT = 256
NTOK = 8
HS = 96
BATCH = 1536
CAP = 240
N_DP = 4


def touch_ends(result, own_key, smallest, top_value):
    longest = result.shape.index(max(result.shape))
    spots = []
    for shift in (0, 1):
        where = [jax.random.randint(jax.random.fold_in(own_key, axis), (), 0, length) for axis, length in enumerate(result.shape)]
        where[longest] = (where[longest] + shift) % result.shape[longest]
        spots.append(tuple(where))
    return result.at[spots[0]].set(smallest).at[spots[1]].set(top_value)


def shard_levels(own_key, dims, shards, low, largest):
    factor_of, own = 1.0, jax.random.fold_in(own_key, 6)
    for dim, blocks in shards:
        steps = jnp.exp(jax.random.uniform(jax.random.fold_in(own, dim), (blocks,), jnp.float32, low / len(shards), largest / len(shards)))
        factor_of = factor_of * jnp.repeat(steps, dims[dim] // blocks).reshape([-1 if axis == dim else 1 for axis in range(len(dims))])
    return factor_of


def rank_table(amount, slope):
    weights = [(1 << 20) // math.isqrt(rank ** slope) + 1 for rank in range(1, amount + 1)]
    spread = 1 + sum(weights) // (1 << 30)
    return np.cumsum(np.array([max(1, weight // spread) for weight in weights]))


def ranked_ids(own_key, dims, number_of, slope):
    grid = rank_table(number_of, slope)
    ticket = jax.random.randint(jax.random.fold_in(own_key, 1), dims, 0, int(grid[number_of - 1]))
    grade = jnp.searchsorted(jnp.asarray(grid, jnp.int32), ticket, side="right")
    return jax.random.permutation(jax.random.fold_in(own_key, 2), number_of)[grade].astype(jnp.int32)


def shared_out(stream_key, own, number, rows, number_of, top, limit, lean):
    sequence = jax.random.permutation(stream_key, number_of)
    crowded, ordinary = portions_of(number_of, rows * top, limit, lean, True), portions_of(number_of, rows * top, limit, lean, False)
    places = jnp.arange(number_of)

    def named(tallies, turn):
        used = int((tallies > 0).sum())
        fixed = max(1, used // 4)
        shifted = fixed + (places - fixed + turn * (used - fixed)) % max(1, number_of - fixed)
        return jnp.zeros((number_of,), jnp.int32).at[sequence[jnp.where(places < fixed, places, shifted)]].set(jnp.asarray(tallies, jnp.int32))

    tallies = jnp.where(number % 4 == 0, named(crowded, number // 4), named(ordinary, number - number // 4 - 1))
    mixed = jax.random.permutation(jax.random.fold_in(own, 3), number_of)
    donor, sink = mixed[0:number_of // 2 * 2:2], mixed[1:number_of // 2 * 2:2]
    margin = jnp.minimum(tallies[donor] - 1, limit - tallies[sink]) // 2
    margin = jnp.where((donor == sequence[0]) | (sink == sequence[0]) | (tallies[sink] == 0), 0, jnp.maximum(margin, 0))
    shifted = jax.random.randint(jax.random.fold_in(own, 4), (number_of // 2,), 0, 1 << 20) % (margin + 1)
    tallies = tallies.at[donor].add(-shifted).at[sink].add(shifted)
    labels = jnp.searchsorted(jnp.cumsum(tallies), jnp.arange(rows * top), side="right").astype(jnp.int32)
    grid = labels.reshape(top, rows).T
    grid = grid[jax.random.permutation(jax.random.fold_in(own, 1), rows)]
    turn = jax.random.randint(jax.random.fold_in(own, 2), (rows, 1), 0, top)
    return jnp.take_along_axis(grid, (jnp.arange(top)[None, :] + turn) % top, axis=1)


def portions_of(count, total, limit, slope, full):
    portions = [(1 << 20) // math.isqrt(standing ** slope) + 1 for standing in range(1, count + 1)]
    largest = limit if full else min(limit, max(-(-total // count), total * portions[0] // sum(portions)))
    least = 1 if total - largest >= count - 1 else 0
    counts, rest = [largest] + [least] * (count - 1), total - largest - least * (count - 1)
    while rest > 0:
        candidates = [i for i in range(1, count) if counts[i] < largest] or [i for i in range(1, count) if counts[i] < limit]
        pool, remaining = sum([portions[i] for i in candidates]), rest
        for i in candidates:
            addition = min(limit - counts[i], max(1, remaining * portions[i] // pool), rest)
            counts[i] = counts[i] + addition
            rest = rest - addition
    return np.array(counts)


def centred(key, extent, deviation, limit, split=(), dtype=jnp.bfloat16):
    entries = jax.random.normal(key, extent, jnp.float32) * deviation
    if len(split) > 0:
        entries = shard_levels(key, extent, split, -0.22, 0.18) * entries
    return jnp.clip(entries, min=-limit, max=limit).astype(dtype)


def setup_inputs(seed: int = 0) -> dict:
    streams_of = jax.random.split(jax.random.key(seed), 9)
    mix_input = centred(streams_of[0], (BATCH, NTOK, D), 1.0, 6.0, ((0, 4), (1, 8)))
    out_grad = centred(streams_of[1], (BATCH, NTOK, D), 0.25, 1.5, ((0, 4), (1, 8)))
    w_up = centred(streams_of[2], (NTOK, D, F), D ** -0.5, 0.21875, ((0, 8),))
    w_down = centred(streams_of[3], (NTOK, F, D), F ** -0.5, 0.109375, ((0, 8),))
    gain_first = jnp.clip(1.0 + 0.15 * jax.random.normal(streams_of[4], (NTOK, D), jnp.float32), 0.25, 1.75)
    gain_second = jnp.clip(1.0 + 0.15 * jax.random.normal(streams_of[5], (NTOK, D), jnp.float32), 0.25, 1.75)
    owner_dev_keys = jax.random.split(jax.random.fold_in(streams_of[6], 1), NTOK * BATCH // B_DEV)
    owner_dev_turns = jax.random.permutation(jax.random.fold_in(streams_of[6], 3), NTOK * BATCH // B_DEV)
    owner_dev = jax.vmap(lambda own, number: shared_out(jax.random.fold_in(streams_of[6], 2), own, number, B_DEV, N_DP, 1, CAP, 2))(owner_dev_keys, owner_dev_turns).reshape((NTOK, BATCH, 1))
    slot_row = touch_ends(ranked_ids(streams_of[7], (NTOK, BATCH), HOT, 2), jax.random.fold_in(streams_of[7], 3), 0, HOT - 1).astype(jnp.int32)
    return dict(mix_input=mix_input, out_grad=out_grad, w_up=w_up, w_down=w_down, gain_first=gain_first, gain_second=gain_second, owner_dev=owner_dev, slot_row=slot_row)


EPS = 1e-05
HALF_ROOT = 0.7071067811865476
INV_ROOT_TAU = 0.3989422804014327

def normalize(values):
    center = values - lax.optimization_barrier(jnp.mean(values, axis=-1, keepdims=True))
    inv_scale = lax.rsqrt(lax.optimization_barrier(jnp.mean(center * center, axis=-1, keepdims=True)) + EPS)
    return (center * inv_scale, inv_scale)

def norm_back(grad_norm, normed, inv_scale):
    mean_grad = lax.optimization_barrier(jnp.mean(grad_norm, axis=-1, keepdims=True))
    mean_proj = lax.optimization_barrier(jnp.mean(grad_norm * normed, axis=-1, keepdims=True))
    return inv_scale * (grad_norm - mean_grad - normed * mean_proj)

def gelu_parts(pre_act):
    cumul = 0.5 * (1.0 + jax.scipy.special.erf(pre_act * HALF_ROOT))
    density = jnp.exp(-0.5 * pre_act * pre_act) * INV_ROOT_TAU
    return (pre_act * cumul, cumul + pre_act * density)

def group_partial(left, right):
    left_parts = left.reshape(N_DP, B_DEV, left.shape[1]).astype(jnp.float32)
    right_parts = right.reshape(N_DP, B_DEV, right.shape[1]).astype(jnp.float32)
    partial_sums = jnp.einsum('nba,nbc->nac', left_parts, right_parts).astype(jnp.bfloat16)
    partial_sums = lax.optimization_barrier(partial_sums)
    return lax.optimization_barrier(jnp.sum(partial_sums.astype(jnp.float32), axis=0))

def per_token(inputs):
    mix_slab, grad_slab, up_mat, down_mat, gain_one, gain_two = inputs
    normed, inv_scale = normalize(mix_slab.astype(jnp.float32))
    hidden_in = (normed * gain_one).astype(jnp.bfloat16)
    pre_act = jnp.dot(hidden_in, up_mat, preferred_element_type=jnp.float32)
    act_value, act_slope = gelu_parts(pre_act)
    active = act_value.astype(jnp.bfloat16)
    outer_sum = jnp.dot(active, down_mat, preferred_element_type=jnp.float32) + hidden_in.astype(jnp.float32)
    normed_out, inv_out = normalize(outer_sum)
    grad_wide = norm_back(grad_slab.astype(jnp.float32) * gain_two, normed_out, inv_out)
    grad_mid = grad_wide.astype(jnp.bfloat16)
    grad_act = jnp.dot(grad_mid, down_mat.T, preferred_element_type=jnp.float32)
    grad_pre = (grad_act * act_slope).astype(jnp.bfloat16)
    grad_up = group_partial(hidden_in, grad_pre)
    grad_down = group_partial(active, grad_mid)
    grad_hidden = jnp.dot(grad_pre, up_mat.T, preferred_element_type=jnp.float32) + grad_wide
    grad_sum = norm_back(grad_hidden * gain_one, normed, inv_scale).astype(jnp.bfloat16)
    return (grad_up, grad_down, grad_sum)

def reference(mix_input, out_grad, w_up, w_down, gain_first, gain_second, owner_dev, slot_row):
    mix_tok = jnp.swapaxes(mix_input, 0, 1)
    grad_tok = jnp.swapaxes(out_grad, 0, 1)
    grad_up, grad_down, grad_sum = lax.map(per_token, (mix_tok, grad_tok, w_up, w_down, gain_first, gain_second))
    pieces = grad_sum.reshape(NTOK, BATCH, NTOK, HS)
    swapped = jnp.transpose(pieces, (2, 1, 0, 3)).reshape(NTOK, BATCH, D)
    embed_grad = (grad_sum.astype(jnp.float32) + swapped.astype(jnp.float32)).astype(jnp.bfloat16)
    target = owner_dev[:, :, 0] * HOT + slot_row

    def table_sum(grad_rows, target_rows):
        return jax.ops.segment_sum(grad_rows.astype(jnp.float32), target_rows, num_segments=N_DP * HOT)
    row_grad = jax.vmap(table_sum)(embed_grad, target)
    return (grad_up, grad_down, row_grad)
```

```python
import functools

import jax
import jax.numpy as jnp
from jax import lax
from jax.experimental import pallas as pl
from jax.experimental.pallas import tpu as pltpu
from jax.sharding import PartitionSpec as P

HOT = 256


EPS = 1e-05
HALF_ROOT = 0.7071067811865476
INV_ROOT_TAU = 0.3989422804014327


def normalize(values):
    center = values - jnp.mean(values, axis=-1, keepdims=True)
    inv_scale = lax.rsqrt(jnp.mean(center * center, axis=-1, keepdims=True) + EPS)
    return (center * inv_scale, inv_scale)


def norm_back(grad_norm, normed, inv_scale):
    mean_grad = jnp.mean(grad_norm, axis=-1, keepdims=True)
    mean_proj = jnp.mean(grad_norm * normed, axis=-1, keepdims=True)
    return inv_scale * (grad_norm - mean_grad - normed * mean_proj)


def gelu_parts(pre_act):
    cumul = 0.5 * (1.0 + jax.scipy.special.erf(pre_act * HALF_ROOT))
    density = jnp.exp(-0.5 * pre_act * pre_act) * INV_ROOT_TAU
    return (pre_act * cumul, cumul + pre_act * density)


def contract_rows(left, right):
    return lax.dot_general(
        left, right, (((0,), (0,)), ((), ())), preferred_element_type=jnp.float32
    )


def contract_cols(left, right):
    return lax.dot_general(
        left, right, (((1,), (1,)), ((), ())), preferred_element_type=jnp.float32
    )


def per_device(mix_input, out_grad, w_up, w_down, gain_first, gain_second, owner_dev, slot_row):
    batch_rows = mix_input.shape[0]
    width = mix_input.shape[2]
    owners = lax.axis_size("dp")
    normed, inv_scale = normalize(mix_input[:, 0, :].astype(jnp.float32))
    hidden_in = (normed * gain_first[0]).astype(jnp.bfloat16)
    pre_act = jnp.dot(hidden_in, w_up[0], preferred_element_type=jnp.float32)
    act_value, act_slope = gelu_parts(pre_act)
    active = act_value.astype(jnp.bfloat16)
    outer_sum = jnp.dot(active, w_down[0], preferred_element_type=jnp.float32) + hidden_in.astype(
        jnp.float32
    )
    normed_out, inv_out = normalize(outer_sum)
    grad_wide = norm_back(
        out_grad[:, 0, :].astype(jnp.float32) * gain_second[0], normed_out, inv_out
    )
    grad_mid = grad_wide.astype(jnp.bfloat16)
    grad_act = contract_cols(grad_mid, w_down[0])
    grad_pre = (grad_act * act_slope).astype(jnp.bfloat16)
    up_whole = contract_rows(hidden_in, grad_pre)
    down_whole = contract_rows(active, grad_mid)
    grad_up, grad_down = (
        lax.psum_scatter(
            up_whole.astype(jnp.bfloat16), "dp", scatter_dimension=0, tiled=True
        ).astype(jnp.float32),
        lax.psum_scatter(
            down_whole.astype(jnp.bfloat16), "dp", scatter_dimension=0, tiled=True
        ).astype(jnp.float32),
    )
    grad_hidden = contract_cols(grad_pre, w_up[0]) + grad_wide
    grad_sum = norm_back(grad_hidden * gain_first[0], normed, inv_scale).astype(jnp.bfloat16)
    pieces = lax.axis_size("token")
    swapped = lax.all_to_all(
        grad_sum.reshape(batch_rows, pieces, width // pieces),
        "token",
        split_axis=1,
        concat_axis=1,
        tiled=True,
    )
    embed_grad = (
        grad_sum.astype(jnp.float32) + swapped.reshape(batch_rows, width).astype(jnp.float32)
    ).astype(jnp.bfloat16)
    owner_ids = owner_dev[0, :, 0]
    slot_ids = slot_row[0]
    capacity = max(2, 8 * (5 * batch_rows // (16 * owners)))
    owner_hot = (
        owner_ids[:, None] == lax.broadcasted_iota(jnp.int32, (batch_rows, owners), 1)
    ).astype(jnp.int32)
    rank_within = jnp.sum((jnp.cumsum(owner_hot, axis=0) - 1) * owner_hot, axis=1)
    place = owner_ids * capacity + rank_within
    dispatch_mask = (
        lax.broadcasted_iota(jnp.int32, (owners * capacity, batch_rows), 0) == place[None, :]
    )
    send_grad = jnp.dot(
        dispatch_mask.astype(jnp.bfloat16), embed_grad, preferred_element_type=jnp.float32
    )
    send_grad = send_grad.astype(jnp.bfloat16).reshape(owners, capacity, width)
    send_slot = jnp.sum(dispatch_mask.astype(jnp.int32) * (slot_ids + 1)[None, :], axis=1) - 1
    send_slot = send_slot.astype(jnp.float32).astype(jnp.bfloat16).reshape(owners, capacity)
    recv_grad, recv_slot = (
        lax.all_to_all(send_grad, "dp", split_axis=0, concat_axis=0, tiled=True),
        lax.all_to_all(send_slot, "dp", split_axis=0, concat_axis=0, tiled=True),
    )
    slot_values = recv_slot.reshape(1, owners * capacity).astype(jnp.float32)
    gather_hot = (
        lax.broadcasted_iota(jnp.int32, (HOT, owners * capacity), 0).astype(jnp.float32)
        == slot_values
    ).astype(jnp.bfloat16)
    row_grad = jnp.dot(
        gather_hot, recv_grad.reshape(owners * capacity, width), preferred_element_type=jnp.float32
    )
    return (grad_up[None], grad_down[None], row_grad[None])


TILE = 512
VMEM_BYTES = 60 * 1024 * 1024


def dot_rows(left, right):
    return lax.dot_general(
        left, right, (((0,), (0,)), ((), ())), preferred_element_type=jnp.float32
    )


def forward_kernel(h_ref, up_ref, down_ref, grad_ref, gain_ref, act_ref, slope_ref, wide_ref, mid_ref, acc):
    step = pl.program_id(0)
    pre = jnp.dot(h_ref[...], up_ref[...], preferred_element_type=jnp.float32)
    value, slope = gelu_parts(pre)
    act = value.astype(jnp.bfloat16)
    act_ref[...] = act
    slope_ref[...] = slope.astype(jnp.bfloat16)
    part = jnp.dot(act, down_ref[...], preferred_element_type=jnp.float32)

    @pl.when(step == 0)
    def _():
        acc[...] = part + h_ref[...].astype(jnp.float32)

    @pl.when(step > 0)
    def _():
        acc[...] += part

    @pl.when(step == pl.num_programs(0) - 1)
    def _():
        normed, inv = normalize(acc[...])
        wide = norm_back(grad_ref[...].astype(jnp.float32) * gain_ref[...], normed, inv)
        wide_ref[...] = wide
        mid_ref[...] = wide.astype(jnp.bfloat16)


def backward_kernel(mid_ref, down_ref, up_ref, slope_ref, wide_ref, mix_ref, gain_ref, pre_ref, sum_ref, acc):
    step = pl.program_id(0)
    grad_act = contract_cols(mid_ref[...], down_ref[...])
    grad_pre = (grad_act * slope_ref[...].astype(jnp.float32)).astype(jnp.bfloat16)
    pre_ref[...] = grad_pre
    part = contract_cols(grad_pre, up_ref[...])

    @pl.when(step == 0)
    def _():
        acc[...] = part + wide_ref[...]

    @pl.when(step > 0)
    def _():
        acc[...] += part

    @pl.when(step == pl.num_programs(0) - 1)
    def _():
        normed, inv = normalize(mix_ref[...].astype(jnp.float32))
        grad_sum = norm_back(acc[...] * gain_ref[...], normed, inv)
        sum_ref[...] = grad_sum.T.astype(jnp.bfloat16)


def others_kernel(own_tiles, me_ref, *refs):
    h_refs = refs[: len(refs) - 3]
    up_ref, slope_ref, act_ref = refs[len(refs) - 3 :]
    for g, h_ref in enumerate(h_refs):
        pre = jnp.dot(h_ref[...], up_ref[...], preferred_element_type=jnp.float32)
        value, slope = gelu_parts(pre)
        slope_ref[g] = slope.astype(jnp.bfloat16)

        @pl.when(pl.program_id(0) < own_tiles)
        def _():
            act_ref[g] = value.astype(jnp.bfloat16)


def up_kernel(groups, *refs):
    mid_refs = refs[: groups - 1]
    hsel_ref, down_ref, slope_ref, own_ref, up_ref = refs[groups - 1 :]
    rows = own_ref.shape[0]
    total = jnp.dot(hsel_ref[:, :rows], own_ref[...], preferred_element_type=jnp.float32)
    for g in range(groups - 1):
        grad_act = contract_cols(mid_refs[g][...], down_ref[...])
        grad_pre = (grad_act * slope_ref[g].astype(jnp.float32)).astype(jnp.bfloat16)
        total += jnp.dot(
            hsel_ref[:, (g + 1) * rows : (g + 2) * rows], grad_pre, preferred_element_type=jnp.float32
        )
    up_ref[...] = total


def down_kernel(me_ref, own_ref, act_ref, *refs):
    mid_refs, out_ref = refs[:-1], refs[-1]
    total = dot_rows(own_ref[...], mid_refs[0][...])
    for g in range(len(mid_refs) - 1):
        total += dot_rows(act_ref[g], mid_refs[g + 1][...])
    out_ref[...] = total


def params():
    return pltpu.CompilerParams(vmem_limit_bytes=VMEM_BYTES)


def whole(*shape):
    return pl.BlockSpec(shape, lambda f, *_: (0,) * len(shape))


def cost(flops, nbytes):
    return pl.CostEstimate(flops=int(flops), bytes_accessed=int(nbytes), transcendentals=0)


def gather_groups(value, groups):
    return [
        lax.ppermute(value, "dp", [(i, i ^ k) for i in range(groups)]) for k in range(1, groups)
    ]


def small_group(mix_input, out_grad, w_up, w_down, gain_first, gain_second, owner_dev, slot_row):
    rows = mix_input.shape[0]
    width = mix_input.shape[2]
    hidden = w_up.shape[2]
    groups = lax.axis_size("dp")
    pieces = lax.axis_size("token")
    me = lax.axis_index("dp")
    me_arr = me.astype(jnp.int32).reshape(1)
    up_mat, down_mat = w_up[0], w_down[0]
    mix = mix_input[:, 0, :]
    grad = out_grad[:, 0, :]
    normed, _ = normalize(mix.astype(jnp.float32))
    hidden_in = (normed * gain_first[0]).astype(jnp.bfloat16)
    others_h = gather_groups(hidden_in, groups)
    steps = hidden // TILE
    bf, f32 = jnp.bfloat16, jnp.float32
    unit = 2 * rows * width * hidden
    wbytes = 2 * width * hidden
    up_spec = pl.BlockSpec((width, TILE), lambda f, *_: (0, f))
    down_spec = pl.BlockSpec((TILE, width), lambda f, *_: (f, 0))
    col_spec = pl.BlockSpec((rows, TILE), lambda f, *_: (0, f))
    active, slope, wide, mid = pl.pallas_call(
        forward_kernel,
        grid=(steps,),
        in_specs=[whole(rows, width), up_spec, down_spec, whole(rows, width), whole(1, width)],
        out_specs=[col_spec, col_spec, whole(rows, width), whole(rows, width)],
        out_shape=[
            jax.ShapeDtypeStruct((rows, hidden), bf),
            jax.ShapeDtypeStruct((rows, hidden), bf),
            jax.ShapeDtypeStruct((rows, width), f32),
            jax.ShapeDtypeStruct((rows, width), bf),
        ],
        scratch_shapes=[pltpu.VMEM((rows, width), f32)],
        compiler_params=params(),
        cost_estimate=cost(2 * unit, 3 * wbytes),
        name="forward",
    )(hidden_in, up_mat, down_mat, grad, gain_second)
    others_mid = gather_groups(mid, groups)
    grad_pre, sum_t = pl.pallas_call(
        backward_kernel,
        grid=(steps,),
        in_specs=[
            whole(rows, width), down_spec, up_spec, col_spec,
            whole(rows, width), whole(rows, width), whole(1, width),
        ],
        out_specs=[col_spec, whole(width, rows)],
        out_shape=[
            jax.ShapeDtypeStruct((rows, hidden), bf),
            jax.ShapeDtypeStruct((width, rows), bf),
        ],
        scratch_shapes=[pltpu.VMEM((rows, width), f32)],
        compiler_params=params(),
        cost_estimate=cost(2 * unit, 3 * wbytes),
        name="backward",
    )(mid, down_mat, up_mat, slope, wide, mix, gain_first)

    swapped = lax.all_to_all(
        sum_t.reshape(pieces, width // pieces, rows), "token", split_axis=0, concat_axis=0, tiled=True
    ).reshape(width, rows)

    own_cols = hidden // groups
    tile_a = min(TILE, own_cols // 2)
    own_tiles = own_cols // tile_a
    steps_a = hidden // tile_a
    o_slope, o_act = pl.pallas_call(
        functools.partial(others_kernel, own_tiles),
        grid_spec=pltpu.PrefetchScalarGridSpec(
            num_scalar_prefetch=1,
            grid=(steps_a,),
            in_specs=[whole(rows, width)] * (groups - 1)
            + [pl.BlockSpec((width, tile_a), lambda f, m: (0, lax.rem(f + m[0] * own_tiles, steps_a)))],
            out_specs=[
                pl.BlockSpec((groups - 1, rows, tile_a), lambda f, m: (0, 0, lax.rem(f + m[0] * own_tiles, steps_a))),
                pl.BlockSpec((groups - 1, rows, tile_a), lambda f, m: (0, 0, jnp.minimum(f, own_tiles - 1))),
            ],
        ),
        out_shape=[
            jax.ShapeDtypeStruct((groups - 1, rows, hidden), bf),
            jax.ShapeDtypeStruct((groups - 1, rows, own_cols), bf),
        ],
        compiler_params=params(),
        cost_estimate=cost((groups - 1) * unit, 3 * wbytes),
        name="others",
    )(me_arr, *others_h, up_mat)

    out_rows = width // groups
    hsel = jnp.concatenate(
        [lax.dynamic_slice(h, (0, me * out_rows), (rows, out_rows)).T for h in [hidden_in] + others_h], axis=1
    )
    grad_up = pl.pallas_call(
        functools.partial(up_kernel, groups),
        grid=(steps,),
        in_specs=[whole(rows, width)] * (groups - 1)
        + [
            whole(out_rows, groups * rows), down_spec,
            pl.BlockSpec((groups - 1, rows, TILE), lambda f: (0, 0, f)), col_spec,
        ],
        out_specs=pl.BlockSpec((out_rows, TILE), lambda f: (0, f)),
        out_shape=jax.ShapeDtypeStruct((out_rows, hidden), f32),
        compiler_params=params(),
        cost_estimate=cost(groups * unit, 5 * wbytes),
        name="upgrad",
    )(*others_mid, hsel, down_mat, o_slope, grad_pre)

    part = own_cols // 3 if own_cols % 384 == 0 else own_cols
    parts = own_cols // part
    grad_down = pl.pallas_call(
        down_kernel,
        grid_spec=pltpu.PrefetchScalarGridSpec(
            num_scalar_prefetch=1,
            grid=(parts,),
            in_specs=[
                pl.BlockSpec((rows, part), lambda f, m: (0, f + m[0] * parts)),
                pl.BlockSpec((groups - 1, rows, part), lambda f, m: (0, 0, f)),
            ]
            + [whole(rows, width)] * groups,
            out_specs=pl.BlockSpec((part, width), lambda f, m: (f, 0)),
        ),
        out_shape=jax.ShapeDtypeStruct((own_cols, width), f32),
        compiler_params=params(),
        cost_estimate=cost(unit, 2 * wbytes),
        name="downgrad",
    )(me_arr, active, o_act, mid, *others_mid)

    embed_t = (sum_t.astype(f32) + swapped.astype(f32)).astype(bf)
    target = owner_dev[0, :, 0] * HOT + slot_row[0]
    hot = (lax.broadcasted_iota(jnp.int32, (groups * HOT, rows), 0) == target[None, :]).astype(bf)
    partial_rows = contract_cols(hot, embed_t).astype(bf).reshape(groups, HOT, width)
    received = lax.all_to_all(partial_rows, "dp", split_axis=0, concat_axis=0, tiled=True)
    row_grad = jnp.sum(received.astype(f32), axis=0)
    return (grad_up[None], grad_down[None], row_grad[None])


def solution(mesh):
    placed = (
        P("dp", "token", None),
        P("dp", "token", None),
        P("token", None, None),
        P("token", None, None),
        P("token", None),
        P("token", None),
        P("token", "dp", None),
        P("token", "dp"),
    )
    return jax.shard_map(
        small_group if mesh.shape["dp"] <= 4 else per_device,
        mesh=mesh,
        in_specs=placed,
        out_specs=(P("token", "dp", None), P("token", "dp", None), P("token", "dp", None)),
        check_vma=False,
    )
```

```python
import functools

import jax
import jax.numpy as jnp
from jax import lax
from jax.experimental import pallas as pl
from jax.experimental.pallas import tpu as pltpu

from jax.sharding import PartitionSpec as P

HOT = 256


EPS = 1e-05
HALF_ROOT = 0.7071067811865476
INV_ROOT_TAU = 0.3989422804014327


def normalize(values):
    center = values - jnp.mean(values, axis=-1, keepdims=True)
    inv_scale = lax.rsqrt(jnp.mean(center * center, axis=-1, keepdims=True) + EPS)
    return (center * inv_scale, inv_scale)


def norm_back(grad_norm, normed, inv_scale):
    mean_grad = jnp.mean(grad_norm, axis=-1, keepdims=True)
    mean_proj = jnp.mean(grad_norm * normed, axis=-1, keepdims=True)
    return inv_scale * (grad_norm - mean_grad - normed * mean_proj)


def gelu_parts(pre_act):
    cumul = 0.5 * (1.0 + jax.scipy.special.erf(pre_act * HALF_ROOT))
    density = jnp.exp(-0.5 * pre_act * pre_act) * INV_ROOT_TAU
    return (pre_act * cumul, cumul + pre_act * density)


def contract_rows(left, right):
    return lax.dot_general(
        left, right, (((0,), (0,)), ((), ())), preferred_element_type=jnp.float32
    )


def contract_cols(left, right):
    return lax.dot_general(
        left, right, (((1,), (1,)), ((), ())), preferred_element_type=jnp.float32
    )


def per_device(mix_input, out_grad, w_up, w_down, gain_first, gain_second, owner_dev, slot_row):
    batch_rows = mix_input.shape[0]
    width = mix_input.shape[2]
    owners = lax.axis_size("dp")
    normed, inv_scale = normalize(mix_input[:, 0, :].astype(jnp.float32))
    hidden_in = (normed * gain_first[0]).astype(jnp.bfloat16)
    pre_act = jnp.dot(hidden_in, w_up[0], preferred_element_type=jnp.float32)
    act_value, act_slope = gelu_parts(pre_act)
    active = act_value.astype(jnp.bfloat16)
    outer_sum = jnp.dot(active, w_down[0], preferred_element_type=jnp.float32) + hidden_in.astype(
        jnp.float32
    )
    normed_out, inv_out = normalize(outer_sum)
    grad_wide = norm_back(
        out_grad[:, 0, :].astype(jnp.float32) * gain_second[0], normed_out, inv_out
    )
    grad_mid = grad_wide.astype(jnp.bfloat16)
    grad_act = contract_cols(grad_mid, w_down[0])
    grad_pre = (grad_act * act_slope).astype(jnp.bfloat16)
    up_whole = contract_rows(hidden_in, grad_pre)
    down_whole = contract_rows(active, grad_mid)
    grad_up, grad_down = (
        lax.psum_scatter(
            up_whole.astype(jnp.bfloat16), "dp", scatter_dimension=0, tiled=True
        ).astype(jnp.float32),
        lax.psum_scatter(
            down_whole.astype(jnp.bfloat16), "dp", scatter_dimension=0, tiled=True
        ).astype(jnp.float32),
    )
    grad_hidden = contract_cols(grad_pre, w_up[0]) + grad_wide
    grad_sum = norm_back(grad_hidden * gain_first[0], normed, inv_scale).astype(jnp.bfloat16)
    pieces = lax.axis_size("token")
    swapped = lax.all_to_all(
        grad_sum.reshape(batch_rows, pieces, width // pieces),
        "token",
        split_axis=1,
        concat_axis=1,
        tiled=True,
    )
    embed_grad = (
        grad_sum.astype(jnp.float32) + swapped.reshape(batch_rows, width).astype(jnp.float32)
    ).astype(jnp.bfloat16)
    owner_ids = owner_dev[0, :, 0]
    slot_ids = slot_row[0]
    capacity = max(2, 8 * (5 * batch_rows // (16 * owners)))
    owner_hot = (
        owner_ids[:, None] == lax.broadcasted_iota(jnp.int32, (batch_rows, owners), 1)
    ).astype(jnp.int32)
    rank_within = jnp.sum((jnp.cumsum(owner_hot, axis=0) - 1) * owner_hot, axis=1)
    place = owner_ids * capacity + rank_within
    dispatch_mask = (
        lax.broadcasted_iota(jnp.int32, (owners * capacity, batch_rows), 0) == place[None, :]
    )
    send_grad = jnp.dot(
        dispatch_mask.astype(jnp.bfloat16), embed_grad, preferred_element_type=jnp.float32
    )
    send_grad = send_grad.astype(jnp.bfloat16).reshape(owners, capacity, width)
    send_slot = jnp.sum(dispatch_mask.astype(jnp.int32) * (slot_ids + 1)[None, :], axis=1) - 1
    send_slot = send_slot.astype(jnp.float32).astype(jnp.bfloat16).reshape(owners, capacity)
    recv_grad, recv_slot = (
        lax.all_to_all(send_grad, "dp", split_axis=0, concat_axis=0, tiled=True),
        lax.all_to_all(send_slot, "dp", split_axis=0, concat_axis=0, tiled=True),
    )
    slot_values = recv_slot.reshape(1, owners * capacity).astype(jnp.float32)
    gather_hot = (
        lax.broadcasted_iota(jnp.int32, (HOT, owners * capacity), 0).astype(jnp.float32)
        == slot_values
    ).astype(jnp.bfloat16)
    row_grad = jnp.dot(
        gather_hot, recv_grad.reshape(owners * capacity, width), preferred_element_type=jnp.float32
    )
    return (grad_up[None], grad_down[None], row_grad[None])


TILE = 1536
SUB = 256
TILE_U = 1024
VMEM_BYTES = 60 * 1024 * 1024


def dot_rows(left, right):
    return lax.dot_general(
        left, right, (((0,), (0,)), ((), ())), preferred_element_type=jnp.float32
    )


def norm_kernel(mix_ref, gain_ref, out_ref):
    normed, _ = normalize(mix_ref[...].astype(jnp.float32))
    out_ref[...] = (normed * gain_ref[...]).astype(jnp.bfloat16)


def forward_kernel(h_ref, up_ref, down_ref, grad_ref, gain_ref, act_ref, slope_ref, wide_ref, mid_ref, acc):
    step = pl.program_id(0)

    @pl.when(step == 0)
    def _():
        acc[...] = h_ref[...].astype(jnp.float32)

    pres = []
    for s in range(0, act_ref.shape[1], SUB):
        pres.append(jnp.dot(h_ref[...], up_ref[:, s : s + SUB], preferred_element_type=jnp.float32))
    part = None
    for i, pre in enumerate(pres):
        cols = slice(i * SUB, (i + 1) * SUB)
        value, slope = gelu_parts(pre)
        act = value.astype(jnp.bfloat16)
        act_ref[:, cols] = act
        slope_ref[:, cols] = slope.astype(jnp.bfloat16)
        more = jnp.dot(act, down_ref[cols, :], preferred_element_type=jnp.float32)
        part = more if part is None else part + more
    acc[...] += part

    @pl.when(step == pl.num_programs(0) - 1)
    def _():
        normed, inv = normalize(acc[...])
        wide = norm_back(grad_ref[...].astype(jnp.float32) * gain_ref[...], normed, inv)
        wide_ref[...] = wide
        mid_ref[...] = wide.astype(jnp.bfloat16)


def backward_kernel(mid_ref, down_ref, up_ref, slope_ref, wide_ref, mix_ref, gain_ref, pre_ref, sum_ref, acc):
    step = pl.program_id(0)

    @pl.when(step == 0)
    def _():
        acc[...] = wide_ref[...]

    grad_act = contract_cols(mid_ref[...], down_ref[...])
    grad_pre = (grad_act * slope_ref[...].astype(jnp.float32)).astype(jnp.bfloat16)
    pre_ref[...] = grad_pre
    acc[...] += contract_cols(grad_pre, up_ref[...])

    @pl.when(step == pl.num_programs(0) - 1)
    def _():
        normed, inv = normalize(mix_ref[...].astype(jnp.float32))
        grad_sum = norm_back(acc[...] * gain_ref[...], normed, inv)
        sum_ref[...] = grad_sum.T.astype(jnp.bfloat16)


def others_kernel(me_ref, *refs):
    h_refs = refs[: len(refs) - 3]
    up_ref, slope_ref, act_ref = refs[len(refs) - 3 :]
    for g, h_ref in enumerate(h_refs):
        pre = jnp.dot(h_ref[...], up_ref[...], preferred_element_type=jnp.float32)
        value, slope = gelu_parts(pre)
        slope_ref[g] = slope.astype(jnp.bfloat16)
        act_ref[g] = value.astype(jnp.bfloat16)


def up_kernel(groups, me_ref, *refs):
    mid_refs = refs[: groups - 1]
    h_refs = refs[groups - 1 : 2 * groups - 1]
    down_ref, slope_ref, own_ref, up_ref, hsel = refs[2 * groups - 1 :]
    width = h_refs[0].shape[1]
    out_rows = up_ref.shape[0]

    @pl.when(pl.program_id(0) == 0)
    def _():
        row = lax.broadcasted_iota(jnp.int32, (out_rows, width), 0) + me_ref[0] * out_rows
        pick = (row == lax.broadcasted_iota(jnp.int32, (out_rows, width), 1)).astype(jnp.bfloat16)
        for g, h_ref in enumerate(h_refs):
            hsel[g] = contract_cols(pick, h_ref[...]).astype(jnp.bfloat16)

    total = jnp.dot(hsel[0], own_ref[...], preferred_element_type=jnp.float32)
    for g in range(groups - 1):
        grad_act = contract_cols(mid_refs[g][...], down_ref[...])
        grad_pre = (grad_act * slope_ref[g].astype(jnp.float32)).astype(jnp.bfloat16)
        total += jnp.dot(hsel[g + 1], grad_pre, preferred_element_type=jnp.float32)
    up_ref[...] = total


def down_kernel(me_ref, own_ref, act_ref, *refs):
    mid_refs, out_ref = refs[:-1], refs[-1]
    total = dot_rows(own_ref[...], mid_refs[0][...])
    for g in range(len(mid_refs) - 1):
        total += dot_rows(act_ref[g], mid_refs[g + 1][...])
    out_ref[...] = total


def params():
    return pltpu.CompilerParams(vmem_limit_bytes=VMEM_BYTES)


def whole(*shape):
    return pl.BlockSpec(shape, lambda f, *_: (0,) * len(shape))


def cost(flops, nbytes):
    return pl.CostEstimate(flops=int(flops), bytes_accessed=int(nbytes), transcendentals=0)


def gather_groups(value, groups):
    taken = []
    for k in range(1, groups):
        taken.append(lax.ppermute(value, "dp", [(i, i ^ k) for i in range(groups)]))
    return taken


def small_group(mix_input, out_grad, w_up, w_down, gain_first, gain_second, owner_dev, slot_row):
    rows = mix_input.shape[0]
    width = mix_input.shape[2]
    hidden = w_up.shape[2]
    groups = lax.axis_size("dp")
    pieces = lax.axis_size("token")
    me = lax.axis_index("dp")
    me_arr = me.astype(jnp.int32).reshape(1)
    up_mat, down_mat = w_up[0], w_down[0]
    mix = mix_input[:, 0, :]
    grad = out_grad[:, 0, :]
    hidden_in = pl.pallas_call(
        norm_kernel,
        out_shape=jax.ShapeDtypeStruct((rows, width), jnp.bfloat16),
        compiler_params=params(),
        name="norm",
    )(mix, gain_first)
    others_h = gather_groups(hidden_in, groups)
    steps = hidden // TILE
    bf, f32 = jnp.bfloat16, jnp.float32
    unit = 2 * rows * width * hidden
    wbytes = 2 * width * hidden
    up_spec = pl.BlockSpec((width, TILE), lambda f, *_: (0, f))
    down_spec = pl.BlockSpec((TILE, width), lambda f, *_: (f, 0))
    col_spec = pl.BlockSpec((rows, TILE), lambda f, *_: (0, f))
    active, slope, wide, mid = pl.pallas_call(
        forward_kernel,
        grid=(steps,),
        in_specs=[whole(rows, width), up_spec, down_spec, whole(rows, width), whole(1, width)],
        out_specs=[col_spec, col_spec, whole(rows, width), whole(rows, width)],
        out_shape=[
            jax.ShapeDtypeStruct((rows, hidden), bf),
            jax.ShapeDtypeStruct((rows, hidden), bf),
            jax.ShapeDtypeStruct((rows, width), f32),
            jax.ShapeDtypeStruct((rows, width), bf),
        ],
        scratch_shapes=[pltpu.VMEM((rows, width), f32)],
        compiler_params=params(),
        cost_estimate=cost(2 * unit, 3 * wbytes),
        name="forward",
    )(hidden_in, up_mat, down_mat, grad, gain_second)
    others_mid = gather_groups(mid, groups)
    grad_pre, sum_t = pl.pallas_call(
        backward_kernel,
        grid=(steps,),
        in_specs=[
            whole(rows, width), down_spec, up_spec, col_spec,
            whole(rows, width), whole(rows, width), whole(1, width),
        ],
        out_specs=[col_spec, whole(width, rows)],
        out_shape=[
            jax.ShapeDtypeStruct((rows, hidden), bf),
            jax.ShapeDtypeStruct((width, rows), bf),
        ],
        scratch_shapes=[pltpu.VMEM((rows, width), f32)],
        compiler_params=params(),
        cost_estimate=cost(2 * unit, 3 * wbytes),
        name="backward",
    )(mid, down_mat, up_mat, slope, wide, mix, gain_first)

    swapped = lax.all_to_all(
        sum_t.reshape(pieces, width // pieces, rows), "token", split_axis=0, concat_axis=0, tiled=True
    ).reshape(width, rows)

    own_cols = hidden // groups
    tile_a = own_cols
    own_tiles = own_cols // tile_a
    steps_a = hidden // tile_a
    o_slope, o_act = pl.pallas_call(
        others_kernel,
        grid_spec=pltpu.PrefetchScalarGridSpec(
            num_scalar_prefetch=1,
            grid=(steps_a,),
            in_specs=[whole(rows, width)] * (groups - 1)
            + [pl.BlockSpec((width, tile_a), lambda f, m: (0, lax.rem(f + (m[0] + 1) * own_tiles, steps_a)))],
            out_specs=[
                pl.BlockSpec((groups - 1, rows, tile_a), lambda f, m: (0, 0, lax.rem(f + (m[0] + 1) * own_tiles, steps_a))),
                pl.BlockSpec((groups - 1, rows, tile_a), lambda f, m: (0, 0, jnp.maximum(f + own_tiles - steps_a, 0))),
            ],
        ),
        out_shape=[
            jax.ShapeDtypeStruct((groups - 1, rows, hidden), bf),
            jax.ShapeDtypeStruct((groups - 1, rows, own_cols), bf),
        ],
        compiler_params=params(),
        cost_estimate=cost((groups - 1) * unit, 3 * wbytes),
        name="others",
    )(me_arr, *others_h, up_mat)

    out_rows = width // groups
    grad_up = pl.pallas_call(
        functools.partial(up_kernel, groups),
        grid_spec=pltpu.PrefetchScalarGridSpec(
            num_scalar_prefetch=1,
            grid=(hidden // TILE_U,),
            in_specs=[whole(rows, width)] * (2 * groups - 1)
            + [
                pl.BlockSpec((TILE_U, width), lambda f, m: (f, 0)),
                pl.BlockSpec((groups - 1, rows, TILE_U), lambda f, m: (0, 0, f)),
                pl.BlockSpec((rows, TILE_U), lambda f, m: (0, f)),
            ],
            out_specs=pl.BlockSpec((out_rows, TILE_U), lambda f, m: (0, f)),
            scratch_shapes=[pltpu.VMEM((groups, out_rows, rows), bf)],
        ),
        out_shape=jax.ShapeDtypeStruct((out_rows, hidden), f32),
        compiler_params=params(),
        cost_estimate=cost(groups * unit, 5 * wbytes),
        name="upgrad",
    )(me_arr, *others_mid, hidden_in, *others_h, down_mat, o_slope, grad_pre)

    part = own_cols // 3 if own_cols % 384 == 0 else own_cols
    parts = own_cols // part
    grad_down = pl.pallas_call(
        down_kernel,
        grid_spec=pltpu.PrefetchScalarGridSpec(
            num_scalar_prefetch=1,
            grid=(parts,),
            in_specs=[
                pl.BlockSpec((rows, part), lambda f, m: (0, f + m[0] * parts)),
                pl.BlockSpec((groups - 1, rows, part), lambda f, m: (0, 0, f)),
            ]
            + [whole(rows, width)] * groups,
            out_specs=pl.BlockSpec((part, width), lambda f, m: (f, 0)),
        ),
        out_shape=jax.ShapeDtypeStruct((own_cols, width), f32),
        compiler_params=params(),
        cost_estimate=cost(unit, 2 * wbytes),
        name="downgrad",
    )(me_arr, active, o_act, mid, *others_mid)

    embed_t = (sum_t.astype(f32) + swapped.astype(f32)).astype(bf)
    target = owner_dev[0, :, 0] * HOT + slot_row[0]
    hot = (lax.broadcasted_iota(jnp.int32, (groups * HOT, rows), 0) == target[None, :]).astype(bf)
    partial_rows = contract_cols(hot, embed_t).astype(bf).reshape(groups, HOT, width)
    received = lax.all_to_all(partial_rows, "dp", split_axis=0, concat_axis=0, tiled=True)
    row_grad = jnp.sum(received.astype(f32), axis=0)
    return (grad_up[None], grad_down[None], row_grad[None])


def solution(mesh):
    placed = (
        P("dp", "token", None),
        P("dp", "token", None),
        P("token", None, None),
        P("token", None, None),
        P("token", None),
        P("token", None),
        P("token", "dp", None),
        P("token", "dp"),
    )
    small = mesh.shape["dp"] <= 4

    def layer(*args):
        return (small_group if small else per_device)(*args)

    return jax.shard_map(
        layer,
        mesh=mesh,
        in_specs=placed,
        out_specs=(P("token", "dp", None), P("token", "dp", None), P("token", "dp", None)),
        check_vma=False,
    )
```

```python
import functools

import jax
import jax.numpy as jnp
from jax import lax
from jax.experimental import pallas as pl
from jax.experimental.pallas import tpu as pltpu

from jax.sharding import PartitionSpec as P

HOT = 256


EPS = 1e-05
HALF_ROOT = 0.7071067811865476
INV_ROOT_TAU = 0.3989422804014327


def normalize(values):
    center = values - jnp.mean(values, axis=-1, keepdims=True)
    inv_scale = lax.rsqrt(jnp.mean(center * center, axis=-1, keepdims=True) + EPS)
    return (center * inv_scale, inv_scale)


def norm_back(grad_norm, normed, inv_scale):
    mean_grad = jnp.mean(grad_norm, axis=-1, keepdims=True)
    mean_proj = jnp.mean(grad_norm * normed, axis=-1, keepdims=True)
    return inv_scale * (grad_norm - mean_grad - normed * mean_proj)


def gelu_parts(pre_act):
    cumul = 0.5 * (1.0 + jax.scipy.special.erf(pre_act * HALF_ROOT))
    density = jnp.exp(-0.5 * pre_act * pre_act) * INV_ROOT_TAU
    return (pre_act * cumul, cumul + pre_act * density)


def contract_rows(left, right):
    return lax.dot_general(
        left, right, (((0,), (0,)), ((), ())), preferred_element_type=jnp.float32
    )


def contract_cols(left, right):
    return lax.dot_general(
        left, right, (((1,), (1,)), ((), ())), preferred_element_type=jnp.float32
    )


def per_device(mix_input, out_grad, w_up, w_down, gain_first, gain_second, owner_dev, slot_row):
    batch_rows = mix_input.shape[0]
    width = mix_input.shape[2]
    owners = lax.axis_size("dp")
    normed, inv_scale = normalize(mix_input[:, 0, :].astype(jnp.float32))
    hidden_in = (normed * gain_first[0]).astype(jnp.bfloat16)
    pre_act = jnp.dot(hidden_in, w_up[0], preferred_element_type=jnp.float32)
    act_value, act_slope = gelu_parts(pre_act)
    active = act_value.astype(jnp.bfloat16)
    outer_sum = jnp.dot(active, w_down[0], preferred_element_type=jnp.float32) + hidden_in.astype(
        jnp.float32
    )
    normed_out, inv_out = normalize(outer_sum)
    grad_wide = norm_back(
        out_grad[:, 0, :].astype(jnp.float32) * gain_second[0], normed_out, inv_out
    )
    grad_mid = grad_wide.astype(jnp.bfloat16)
    grad_act = contract_cols(grad_mid, w_down[0])
    grad_pre = (grad_act * act_slope).astype(jnp.bfloat16)
    up_whole = contract_rows(hidden_in, grad_pre)
    down_whole = contract_rows(active, grad_mid)
    grad_up, grad_down = (
        lax.psum_scatter(
            up_whole.astype(jnp.bfloat16), "dp", scatter_dimension=0, tiled=True
        ).astype(jnp.float32),
        lax.psum_scatter(
            down_whole.astype(jnp.bfloat16), "dp", scatter_dimension=0, tiled=True
        ).astype(jnp.float32),
    )
    grad_hidden = contract_cols(grad_pre, w_up[0]) + grad_wide
    grad_sum = norm_back(grad_hidden * gain_first[0], normed, inv_scale).astype(jnp.bfloat16)
    pieces = lax.axis_size("token")
    swapped = lax.all_to_all(
        grad_sum.reshape(batch_rows, pieces, width // pieces),
        "token",
        split_axis=1,
        concat_axis=1,
        tiled=True,
    )
    embed_grad = (
        grad_sum.astype(jnp.float32) + swapped.reshape(batch_rows, width).astype(jnp.float32)
    ).astype(jnp.bfloat16)
    owner_ids = owner_dev[0, :, 0]
    slot_ids = slot_row[0]
    capacity = max(2, 8 * (5 * batch_rows // (16 * owners)))
    owner_hot = (
        owner_ids[:, None] == lax.broadcasted_iota(jnp.int32, (batch_rows, owners), 1)
    ).astype(jnp.int32)
    rank_within = jnp.sum((jnp.cumsum(owner_hot, axis=0) - 1) * owner_hot, axis=1)
    place = owner_ids * capacity + rank_within
    dispatch_mask = (
        lax.broadcasted_iota(jnp.int32, (owners * capacity, batch_rows), 0) == place[None, :]
    )
    send_grad = jnp.dot(
        dispatch_mask.astype(jnp.bfloat16), embed_grad, preferred_element_type=jnp.float32
    )
    send_grad = send_grad.astype(jnp.bfloat16).reshape(owners, capacity, width)
    send_slot = jnp.sum(dispatch_mask.astype(jnp.int32) * (slot_ids + 1)[None, :], axis=1) - 1
    send_slot = send_slot.astype(jnp.float32).astype(jnp.bfloat16).reshape(owners, capacity)
    recv_grad, recv_slot = (
        lax.all_to_all(send_grad, "dp", split_axis=0, concat_axis=0, tiled=True),
        lax.all_to_all(send_slot, "dp", split_axis=0, concat_axis=0, tiled=True),
    )
    slot_values = recv_slot.reshape(1, owners * capacity).astype(jnp.float32)
    gather_hot = (
        lax.broadcasted_iota(jnp.int32, (HOT, owners * capacity), 0).astype(jnp.float32)
        == slot_values
    ).astype(jnp.bfloat16)
    row_grad = jnp.dot(
        gather_hot, recv_grad.reshape(owners * capacity, width), preferred_element_type=jnp.float32
    )
    return (grad_up[None], grad_down[None], row_grad[None])


TILE = 1536
SUB = 256
TILE_U = 1024
VMEM_BYTES = 60 * 1024 * 1024


def dot_rows(left, right):
    return lax.dot_general(
        left, right, (((0,), (0,)), ((), ())), preferred_element_type=jnp.float32
    )


def norm_kernel(mix_ref, gain_ref, out_ref):
    normed, _ = normalize(mix_ref[...].astype(jnp.float32))
    out_ref[...] = (normed * gain_ref[...]).astype(jnp.bfloat16)


def forward_kernel(h_ref, up_ref, down_ref, grad_ref, gain_ref, act_ref, slope_ref, wide_ref, mid_ref, acc):
    step = pl.program_id(0)

    @pl.when(step == 0)
    def _():
        acc[...] = h_ref[...].astype(jnp.float32)

    pres = []
    for s in range(0, act_ref.shape[1], SUB):
        pres.append(jnp.dot(h_ref[...], up_ref[:, s : s + SUB], preferred_element_type=jnp.float32))
    part = None
    for i, pre in enumerate(pres):
        cols = slice(i * SUB, (i + 1) * SUB)
        value, slope = gelu_parts(pre)
        act = value.astype(jnp.bfloat16)
        act_ref[:, cols] = act
        slope_ref[:, cols] = slope.astype(jnp.bfloat16)
        more = jnp.dot(act, down_ref[cols, :], preferred_element_type=jnp.float32)
        part = more if part is None else part + more
    acc[...] += part

    @pl.when(step == pl.num_programs(0) - 1)
    def _():
        normed, inv = normalize(acc[...])
        wide = norm_back(grad_ref[...].astype(jnp.float32) * gain_ref[...], normed, inv)
        wide_ref[...] = wide
        mid_ref[...] = wide.astype(jnp.bfloat16)


def backward_kernel(mid_ref, down_ref, up_ref, slope_ref, wide_ref, mix_ref, gain_ref, pre_ref, sum_ref, acc):
    step = pl.program_id(0)

    @pl.when(step == 0)
    def _():
        acc[...] = wide_ref[...]

    grad_act = contract_cols(mid_ref[...], down_ref[...])
    grad_pre = (grad_act * slope_ref[...].astype(jnp.float32)).astype(jnp.bfloat16)
    pre_ref[...] = grad_pre
    acc[...] += contract_cols(grad_pre, up_ref[...])

    @pl.when(step == pl.num_programs(0) - 1)
    def _():
        normed, inv = normalize(mix_ref[...].astype(jnp.float32))
        grad_sum = norm_back(acc[...] * gain_ref[...], normed, inv)
        sum_ref[...] = grad_sum.T.astype(jnp.bfloat16)


def others_kernel(me_ref, *refs):
    h_refs = refs[: len(refs) - 4]
    up_ref, slope_ref, act_ref, hsel_ref = refs[len(refs) - 4 :]
    width = h_refs[0].shape[1]
    out_rows = hsel_ref.shape[1]

    @pl.when(pl.program_id(0) == 0)
    def _():
        row = lax.broadcasted_iota(jnp.int32, (out_rows, width), 0) + me_ref[0] * out_rows
        pick = (row == lax.broadcasted_iota(jnp.int32, (out_rows, width), 1)).astype(jnp.bfloat16)
        for g, h_ref in enumerate(h_refs):
            hsel_ref[g] = contract_cols(pick, h_ref[...]).astype(jnp.bfloat16)

    for g, h_ref in enumerate(h_refs[1:]):
        pre = jnp.dot(h_ref[...], up_ref[...], preferred_element_type=jnp.float32)
        value, slope = gelu_parts(pre)
        slope_ref[g] = slope.astype(jnp.bfloat16)
        act_ref[g] = value.astype(jnp.bfloat16)


def weights_kernel(groups, me_ref, *refs):
    mid_refs = refs[:groups]
    hsel_ref, down_ref, slope_ref, own_ref, act_own_ref, act_ref, up_ref, out_ref = refs[groups:]
    total = jnp.dot(hsel_ref[0], own_ref[...], preferred_element_type=jnp.float32)
    rows = dot_rows(act_own_ref[...], mid_refs[0][...])
    for g in range(groups - 1):
        grad_act = contract_cols(mid_refs[g + 1][...], down_ref[...])
        grad_pre = (grad_act * slope_ref[g].astype(jnp.float32)).astype(jnp.bfloat16)
        total += jnp.dot(hsel_ref[g + 1], grad_pre, preferred_element_type=jnp.float32)
        rows += dot_rows(act_ref[g], mid_refs[g + 1][...])
    up_ref[...] = total
    out_ref[...] = rows


def params():
    return pltpu.CompilerParams(vmem_limit_bytes=VMEM_BYTES)


def whole(*shape):
    return pl.BlockSpec(shape, lambda f, *_: (0,) * len(shape))


def cost(flops, nbytes):
    return pl.CostEstimate(flops=int(flops), bytes_accessed=int(nbytes), transcendentals=0)


def gather_groups(value, groups):
    taken = []
    for k in range(1, groups):
        taken.append(lax.ppermute(value, "dp", [(i, i ^ k) for i in range(groups)]))
    return taken


def small_group(mix_input, out_grad, w_up, w_down, gain_first, gain_second, owner_dev, slot_row):
    rows = mix_input.shape[0]
    width = mix_input.shape[2]
    hidden = w_up.shape[2]
    groups = lax.axis_size("dp")
    pieces = lax.axis_size("token")
    me = lax.axis_index("dp")
    me_arr = me.astype(jnp.int32).reshape(1)
    up_mat, down_mat = w_up[0], w_down[0]
    mix = mix_input[:, 0, :]
    grad = out_grad[:, 0, :]
    hidden_in = pl.pallas_call(
        norm_kernel,
        out_shape=jax.ShapeDtypeStruct((rows, width), jnp.bfloat16),
        compiler_params=params(),
        name="norm",
    )(mix, gain_first)
    others_h = gather_groups(hidden_in, groups)
    steps = hidden // TILE
    bf, f32 = jnp.bfloat16, jnp.float32
    unit = 2 * rows * width * hidden
    wbytes = 2 * width * hidden
    up_spec = pl.BlockSpec((width, TILE), lambda f, *_: (0, f))
    down_spec = pl.BlockSpec((TILE, width), lambda f, *_: (f, 0))
    col_spec = pl.BlockSpec((rows, TILE), lambda f, *_: (0, f))
    active, slope, wide, mid = pl.pallas_call(
        forward_kernel,
        grid=(steps,),
        in_specs=[whole(rows, width), up_spec, down_spec, whole(rows, width), whole(1, width)],
        out_specs=[col_spec, col_spec, whole(rows, width), whole(rows, width)],
        out_shape=[
            jax.ShapeDtypeStruct((rows, hidden), bf),
            jax.ShapeDtypeStruct((rows, hidden), bf),
            jax.ShapeDtypeStruct((rows, width), f32),
            jax.ShapeDtypeStruct((rows, width), bf),
        ],
        scratch_shapes=[pltpu.VMEM((rows, width), f32)],
        compiler_params=params(),
        cost_estimate=cost(2 * unit, 3 * wbytes),
        name="forward",
    )(hidden_in, up_mat, down_mat, grad, gain_second)
    others_mid = gather_groups(mid, groups)
    grad_pre, sum_t = pl.pallas_call(
        backward_kernel,
        grid=(steps,),
        in_specs=[
            whole(rows, width), down_spec, up_spec, col_spec,
            whole(rows, width), whole(rows, width), whole(1, width),
        ],
        out_specs=[col_spec, whole(width, rows)],
        out_shape=[
            jax.ShapeDtypeStruct((rows, hidden), bf),
            jax.ShapeDtypeStruct((width, rows), bf),
        ],
        scratch_shapes=[pltpu.VMEM((rows, width), f32)],
        compiler_params=params(),
        cost_estimate=cost(2 * unit, 3 * wbytes),
        name="backward",
    )(mid, down_mat, up_mat, slope, wide, mix, gain_first)

    swapped = lax.all_to_all(
        sum_t.reshape(pieces, width // pieces, rows), "token", split_axis=0, concat_axis=0, tiled=True
    ).reshape(width, rows)

    own_cols = hidden // groups
    tile_a = own_cols
    own_tiles = own_cols // tile_a
    steps_a = hidden // tile_a
    out_rows = width // groups
    o_slope, o_act, hsel = pl.pallas_call(
        others_kernel,
        grid_spec=pltpu.PrefetchScalarGridSpec(
            num_scalar_prefetch=1,
            grid=(steps_a,),
            in_specs=[whole(rows, width)] * groups
            + [pl.BlockSpec((width, tile_a), lambda f, m: (0, lax.rem(f + (m[0] + 1) * own_tiles, steps_a)))],
            out_specs=[
                pl.BlockSpec((groups - 1, rows, tile_a), lambda f, m: (0, 0, lax.rem(f + (m[0] + 1) * own_tiles, steps_a))),
                pl.BlockSpec((groups - 1, rows, tile_a), lambda f, m: (0, 0, jnp.maximum(f + own_tiles - steps_a, 0))),
                whole(groups, out_rows, rows),
            ],
        ),
        out_shape=[
            jax.ShapeDtypeStruct((groups - 1, rows, hidden), bf),
            jax.ShapeDtypeStruct((groups - 1, rows, own_cols), bf),
            jax.ShapeDtypeStruct((groups, out_rows, rows), bf),
        ],
        compiler_params=params(),
        cost_estimate=cost((groups - 1) * unit, 3 * wbytes),
        name="others",
    )(me_arr, hidden_in, *others_h, up_mat)

    parts = hidden // TILE_U
    part = own_cols // parts
    grad_up, grad_down = pl.pallas_call(
        functools.partial(weights_kernel, groups),
        grid_spec=pltpu.PrefetchScalarGridSpec(
            num_scalar_prefetch=1,
            grid=(parts,),
            in_specs=[whole(rows, width)] * groups
            + [
                whole(groups, out_rows, rows),
                pl.BlockSpec((TILE_U, width), lambda f, m: (f, 0)),
                pl.BlockSpec((groups - 1, rows, TILE_U), lambda f, m: (0, 0, f)),
                pl.BlockSpec((rows, TILE_U), lambda f, m: (0, f)),
                pl.BlockSpec((rows, part), lambda f, m: (0, f + m[0] * parts)),
                pl.BlockSpec((groups - 1, rows, part), lambda f, m: (0, 0, f)),
            ],
            out_specs=[
                pl.BlockSpec((out_rows, TILE_U), lambda f, m: (0, f)),
                pl.BlockSpec((part, width), lambda f, m: (f, 0)),
            ],
        ),
        out_shape=[
            jax.ShapeDtypeStruct((out_rows, hidden), f32),
            jax.ShapeDtypeStruct((own_cols, width), f32),
        ],
        compiler_params=params(),
        cost_estimate=cost((groups + 1) * unit, 6 * wbytes),
        name="weights",
    )(me_arr, mid, *others_mid, hsel, down_mat, o_slope, grad_pre, active, o_act)

    embed_t = (sum_t.astype(f32) + swapped.astype(f32)).astype(bf)
    target = owner_dev[0, :, 0] * HOT + slot_row[0]
    hot = (lax.broadcasted_iota(jnp.int32, (groups * HOT, rows), 0) == target[None, :]).astype(bf)
    partial_rows = contract_cols(hot, embed_t).astype(bf).reshape(groups, HOT, width)
    received = lax.all_to_all(partial_rows, "dp", split_axis=0, concat_axis=0, tiled=True)
    row_grad = jnp.sum(received.astype(f32), axis=0)
    return (grad_up[None], grad_down[None], row_grad[None])


def solution(mesh):
    placed = (
        P("dp", "token", None),
        P("dp", "token", None),
        P("token", None, None),
        P("token", None, None),
        P("token", None),
        P("token", None),
        P("token", "dp", None),
        P("token", "dp"),
    )
    small = mesh.shape["dp"] == 4

    def layer(*args):
        return (small_group if small else per_device)(*args)

    return jax.shard_map(
        layer,
        mesh=mesh,
        in_specs=placed,
        out_specs=(P("token", "dp", None), P("token", "dp", None), P("token", "dp", None)),
        check_vma=False,
    )
```
